32 devices in a mesh: row: 8 (over z, core), col: 4 (over y, x).
Axes of the slice: x: 2, y: 2, z: 4, core: 2. Of those that a mesh axis runs over, the one named last changes fastest.
Arguments:
- iterate: bfloat16 [3584, 18432], P('col', 'row'), may hold values from -5.2 to 5.2
Outputs:
- next_iterate: float32 [3584, 18432], P('col', 'row')
The draws below stay inside these ranges and needn't reach their ends.
All inputs are finite; a program needn't handle non-finite values.
Results may differ from the reference program's by a relative error of at most 0.0032.
Values may be sent and summed in bfloat16 or wider, within the bound.
A program may use at most 128 MiB of HBM per device.

```python
import jax
import jax.numpy as jnp

M = 3584
N = 18432


def draw_iterate(key, part):
    key_base, key_level = jax.random.split(key, 2)
    column_group = jnp.arange(N) * 64 // N
    level = jax.random.uniform(key_level, (64,), jnp.float32)
    column_scale = jnp.power(10.0, level)[column_group]
    base = jax.random.truncated_normal(key_base, -4.0, 4.0, (M, N), jnp.float32)
    return (base * column_scale[None, :] * 0.1276).astype(jnp.bfloat16)


def setup_inputs(seed: int = 0) -> dict:
    key_list = jax.random.split(jax.random.key(seed), 2)
    iterate = draw_iterate(jax.random.fold_in(key_list[1], 71), 0)
    return {"iterate": iterate}


QUINTIC_A = 3.4445
QUINTIC_B = -4.7750
QUINTIC_C = 2.0315


def reference(iterate):
    inverse = 1.0 / N
    raw_gram = jnp.dot(iterate, iterate.T, preferred_element_type=jnp.float32)
    gram = (raw_gram * inverse).astype(jnp.bfloat16)
    square = jnp.dot(gram, gram, preferred_element_type=jnp.float32)
    poly = (QUINTIC_B * gram.astype(jnp.float32) + QUINTIC_C * square).astype(jnp.bfloat16)
    product = jnp.dot(poly, iterate, preferred_element_type=jnp.float32)
    return QUINTIC_A * iterate.astype(jnp.float32) + product
```

```python
import functools

import jax
import jax.numpy as jnp
from jax import lax
from jax.experimental import pallas as pl
from jax.experimental.pallas import tpu as pltpu
from jax.sharding import PartitionSpec as P

N = 18432


QUINTIC_A = 3.4445
QUINTIC_B = -4.775
QUINTIC_C = 2.0315

VMEM_LIMIT = 60 * 2**20
ROWS_BY_ROWS = (((1,), (1,)), ((), ()))
COLS_BY_ROWS = (((0,), (0,)), ((), ()))


def general(iterate):
    inverse = 1.0 / N
    column_slab = lax.all_gather(iterate, "col", axis=0, tiled=True)
    gram_total = lax.psum_scatter(
        lax.dot_general(column_slab, iterate, ROWS_BY_ROWS, preferred_element_type=jnp.float32),
        "row",
        scatter_dimension=0,
        tiled=True,
    )
    gram_tile = (gram_total * inverse).astype(jnp.bfloat16)
    row_panel = lax.all_gather(gram_tile, "col", axis=1, tiled=True)
    square = jnp.dot(
        row_panel,
        lax.all_gather(gram_tile, "row", axis=0, tiled=True),
        preferred_element_type=jnp.float32,
    )
    poly_tile = (QUINTIC_B * gram_tile.astype(jnp.float32) + QUINTIC_C * square).astype(
        jnp.bfloat16
    )
    product = lax.dot_general(
        lax.all_gather(poly_tile, "row", axis=0, tiled=True),
        column_slab,
        COLS_BY_ROWS,
        preferred_element_type=jnp.float32,
    )
    return QUINTIC_A * iterate.astype(jnp.float32) + product


def polynomial_kernel(
    depth, inverse, x_ref, slab_out, poly_out,
    slab, part, paired, outgoing, incoming, gram, panel, poly,
    x_send, x_recv, pair_send, pair_recv, sum_send, sum_recv,
    hop_send, hop_recv, side_send, side_recv, panel_send, panel_recv, out_sem,
):
    m = x_ref.shape[0]
    h, s = m // 2, m // (2 * depth)
    c, r = lax.axis_index("col"), lax.axis_index("row")
    z = r // 2
    core = r % 2
    side = r + 1 - 2 * core
    across = {1: c + 1 - 2 * (c % 2), 2: (c + 2) % 4, 3: 3 - c}
    lo, hi = pl.ds(0, h), pl.ds(h, h)

    def remote(source, target, send, recv, row=r, col=c):
        return pltpu.make_async_remote_copy(
            src_ref=source, dst_ref=target, send_sem=send, recv_sem=recv,
            device_id={"row": row, "col": col}, device_id_type=pl.DeviceIdType.MESH,
        )

    barrier = pltpu.get_barrier_semaphore()
    partners = [(r, across[l]) for l in (1, 2, 3)] + [(side, c)]
    partners += [(2 * ((z + d) % depth) + core, c) for d in range(1, depth)]
    for row, col in partners:
        pl.semaphore_signal(
            barrier, inc=1, device_id={"row": row, "col": col},
            device_id_type=pl.DeviceIdType.MESH,
        )
    pl.semaphore_wait(barrier, len(partners))

    def x_copy(i):
        source, block, half, bit = [
            (x_ref, 0, lo, 1),
            (x_ref, 1, hi, 2),
            (x_ref, 0, hi, 1),
            (x_ref, 1, lo, 2),
            (slab.at[0], 2, lo, 2),
            (slab.at[1], 2, hi, 1),
        ][i]
        return remote(
            source.at[half], slab.at[block, half], x_send.at[i], x_recv.at[i], col=across[bit]
        )

    def keep(k):
        source = x_ref if k == 0 else slab.at[k - 1]
        return pltpu.make_async_copy(source, slab_out.at[k], out_sem.at[k])

    def pair_copy(k):
        return remote(
            part.at[k % 2, 1 - core], paired.at[k], pair_send.at[k], pair_recv.at[k], row=side
        )

    def products(k):
        def step(i, carry):
            rows = pl.ds(pl.multiple_of(i * 2 * s, 2 * s), 2 * s)
            block = x_ref[rows] if k == 0 else slab[k - 1, rows]
            total = inverse * lax.dot_general(
                block, x_ref[...], ROWS_BY_ROWS, preferred_element_type=jnp.float32
            )
            part[k % 2, 0, i] = total[:s]
            part[k % 2, 1, i] = total[s:]
            return carry

        lax.fori_loop(0, depth, step, 0)
        pair_copy(k).start()

    def sum_copy(k, d):
        there = (z + d) % depth
        return remote(
            outgoing.at[k, there], incoming.at[k, d - 1],
            sum_send.at[k, d - 1], sum_recv.at[k, d - 1], row=2 * there + core,
        )

    def send_sums(k):
        pair_copy(k).wait_recv()

        def step(i, carry):
            outgoing[k, i] = (part[k % 2, core, i] + paired[k, i]).astype(jnp.bfloat16)
            return carry

        lax.fori_loop(0, depth, step, 0)
        for d in range(1, depth):
            sum_copy(k, d).start()

    def panel_copy(k, l):
        return remote(
            gram.at[k, r], panel.at[l, k ^ l],
            panel_send.at[k, l - 1], panel_recv.at[k, l - 1], col=across[l],
        )

    def finish_sums(k):
        total = part[k % 2, core, z] + paired[k, z]
        for d in range(1, depth):
            sum_copy(k, d).wait_recv()
            total += incoming[k, d - 1].astype(jnp.float32)
        total = total.astype(jnp.bfloat16)
        gram[k, r] = total
        panel[0, k] = total
        spread(0, gram, k)
        for l in (1, 2, 3):
            panel_copy(k, l).start()

    def hop(g, buffer, k, way, d):
        source = r - 2 * (d - 1) if way == 0 else r + 2 * (d - 1)
        target = r + 2 if way == 0 else r - 2
        return remote(
            buffer.at[k, source], buffer.at[k, source],
            hop_send.at[g, k, way, d - 1], hop_recv.at[g, k, way, d - 1], row=target,
        )

    def sends(way, d):
        if way == 0:
            return jnp.logical_and(z - (d - 1) >= 0, z <= depth - 2)
        return jnp.logical_and(z + (d - 1) <= depth - 1, z >= 1)

    def gets(way, d):
        return z - d >= 0 if way == 0 else z + d <= depth - 1

    def side_copy(g, buffer, k, way, d):
        source = r - 2 * d if way == 0 else r + 2 * d
        slot = d if way == 0 else depth - 1 + d
        return remote(
            buffer.at[k, source], buffer.at[k, source],
            side_send.at[g, k, slot], side_recv.at[g, k, slot], row=side,
        )

    def side_arrival(g, buffer, k, way, d):
        source = side - 2 * d if way == 0 else side + 2 * d
        slot = d if way == 0 else depth - 1 + d
        return remote(
            buffer.at[k, source], buffer.at[k, source],
            side_send.at[g, k, slot], side_recv.at[g, k, slot], row=side,
        )

    def arrival(g, buffer, k, way, d):
        source = r - 2 * d if way == 0 else r + 2 * d
        return remote(
            buffer.at[k, source], buffer.at[k, source],
            hop_send.at[g, k, way, d - 1], hop_recv.at[g, k, way, d - 1], row=side,
        )

    def spread(g, buffer, k):
        for way in (0, 1):
            pl.when(sends(way, 1))(lambda way=way: hop(g, buffer, k, way, 1).start())
        side_copy(g, buffer, k, 0, 0).start()

    def pass_on(g, buffer, k, d):
        for way in (0, 1):

            @pl.when(gets(way, d))
            def _(way=way):
                arrival(g, buffer, k, way, d).wait_recv()
                side_copy(g, buffer, k, way, d).start()

            if d < depth - 1:
                pl.when(sends(way, d + 1))(lambda way=way: hop(g, buffer, k, way, d + 1).start())

    def gathered(g, buffer, k):
        side_arrival(g, buffer, k, 0, 0).wait_recv()
        for way in (0, 1):
            for d in range(1, depth):
                pl.when(gets(way, d))(
                    lambda way=way, d=d: side_arrival(g, buffer, k, way, d).wait_recv()
                )

    def spread_sent(g, buffer, k):
        side_copy(g, buffer, k, 0, 0).wait_send()
        for way in (0, 1):
            for d in range(1, depth):
                pl.when(gets(way, d))(
                    lambda way=way, d=d: side_copy(g, buffer, k, way, d).wait_send()
                )
                pl.when(sends(way, d))(
                    lambda way=way, d=d: hop(g, buffer, k, way, d).wait_send()
                )

    x_copy(0).start()
    x_copy(1).start()
    keep(0).start()
    products(0)
    send_sums(0)
    for i in (0, 1):
        x_copy(i).wait()
    x_copy(2).start()
    x_copy(3).start()
    finish_sums(0)
    for d in range(1, depth):
        pass_on(0, gram, 0, d)
    for i in (2, 3):
        x_copy(i).wait()
    x_copy(4).start()
    x_copy(5).start()
    keep(1).start()
    keep(2).start()
    products(1)
    pair_copy(0).wait_send()
    products(2)
    send_sums(1)
    send_sums(2)
    finish_sums(1)
    finish_sums(2)
    for d in range(1, depth):
        pass_on(0, gram, 1, d)
        pass_on(0, gram, 2, d)
    pair_copy(1).wait_send()
    for i in (4, 5):
        x_copy(i).wait()
    keep(3).start()
    products(3)
    send_sums(3)
    finish_sums(3)
    for d in range(1, depth):
        pass_on(0, gram, 3, d)
    for k in range(4):
        for l in (1, 2, 3):
            panel_copy(k, l).wait_recv()
        gathered(0, gram, k)

    for first in (0, 2):
        square = jnp.zeros((2 * s, m), jnp.float32)
        for l in range(4):
            square += jnp.dot(
                panel[l, first : first + 2].reshape(2 * s, m),
                gram[l].reshape(m, m),
                preferred_element_type=jnp.float32,
            )
        for k in (first, first + 1):
            own = panel[0, k].astype(jnp.float32)
            rows = square[(k - first) * s : (k - first + 1) * s]
            poly[k, r] = (QUINTIC_B * own + QUINTIC_C * rows).astype(jnp.bfloat16)
            spread(1, poly, k)
    for d in range(1, depth):
        for k in range(4):
            pass_on(1, poly, k, d)
    for k in range(4):
        gathered(1, poly, k)
        pltpu.make_async_copy(poly.at[k], poly_out.at[k], out_sem.at[4 + k]).start()

    for k in range(4):
        if k > 1:
            pair_copy(k).wait_send()
        for d in range(1, depth):
            sum_copy(k, d).wait_send()
        for l in (1, 2, 3):
            panel_copy(k, l).wait_send()
        spread_sent(0, gram, k)
        spread_sent(1, poly, k)
        keep(k).wait()
        pltpu.make_async_copy(poly.at[k], poly_out.at[k], out_sem.at[4 + k]).wait()


def square_of_four(rows, iterate):
    m, n = iterate.shape
    depth, s = rows // 2, m // rows
    bf16, f32, dma = jnp.bfloat16, jnp.float32, pltpu.SemaphoreType.DMA
    slab, poly = pl.pallas_call(
        functools.partial(polynomial_kernel, depth, 1.0 / N),
        out_shape=(
            jax.ShapeDtypeStruct((4, m, n), bf16),
            jax.ShapeDtypeStruct((4, rows, s, m), bf16),
        ),
        in_specs=[pl.BlockSpec(memory_space=pltpu.VMEM)],
        out_specs=(pl.BlockSpec(memory_space=pl.ANY), pl.BlockSpec(memory_space=pl.ANY)),
        scratch_shapes=[
            pltpu.VMEM((3, m, n), bf16),
            pltpu.VMEM((2, 2, depth, s, m), f32),
            pltpu.VMEM((4, depth, s, m), f32),
            pltpu.VMEM((4, depth, s, m), bf16),
            pltpu.VMEM((4, depth - 1, s, m), bf16),
            pltpu.VMEM((4, rows, s, m), bf16),
            pltpu.VMEM((4, 4, s, m), bf16),
            pltpu.VMEM((4, rows, s, m), bf16),
            dma((6,)), dma((6,)),
            dma((4,)), dma((4,)),
            dma((4, depth - 1)), dma((4, depth - 1)),
            dma((2, 4, 2, depth - 1)), dma((2, 4, 2, depth - 1)),
            dma((2, 4, rows - 1)), dma((2, 4, rows - 1)),
            dma((4, 3)), dma((4, 3)),
            dma((8,)),
        ],
        compiler_params=pltpu.CompilerParams(
            collective_id=0, has_side_effects=True, vmem_limit_bytes=VMEM_LIMIT
        ),
    )(iterate)
    product = lax.dot_general(
        poly.reshape(4 * m, m), slab.reshape(4 * m, n), COLS_BY_ROWS, preferred_element_type=f32
    )
    return QUINTIC_A * iterate.astype(f32) + product


def solution(mesh):
    rows, cols = mesh.shape["row"], mesh.shape["col"]
    placed = (P("col", "row"),)

    def local(iterate):
        m, n = iterate.shape
        if cols == 4 and rows % 2 == 0 and m % (16 * rows) == 0 and 30 * m * m + 10 * m * n < VMEM_LIMIT:
            return square_of_four(rows, iterate)
        return general(iterate)

    return jax.shard_map(
        local, mesh=mesh, in_specs=placed, out_specs=P("col", "row"), check_vma=False
    )
```

```python
import functools

import jax
import jax.numpy as jnp
from jax import lax
from jax.experimental import pallas as pl
from jax.experimental.pallas import tpu as pltpu
from jax.sharding import PartitionSpec as P

N = 18432


QUINTIC_A = 3.4445
QUINTIC_B = -4.775
QUINTIC_C = 2.0315

VMEM_LIMIT = 60 * 2**20
ROWS_BY_ROWS = (((1,), (1,)), ((), ()))
COLS_BY_ROWS = (((0,), (0,)), ((), ()))


def general(iterate):
    inverse = 1.0 / N
    column_slab = lax.all_gather(iterate, "col", axis=0, tiled=True)
    gram_total = lax.psum_scatter(
        lax.dot_general(column_slab, iterate, ROWS_BY_ROWS, preferred_element_type=jnp.float32),
        "row",
        scatter_dimension=0,
        tiled=True,
    )
    gram_tile = (gram_total * inverse).astype(jnp.bfloat16)
    row_panel = lax.all_gather(gram_tile, "col", axis=1, tiled=True)
    square = jnp.dot(
        row_panel,
        lax.all_gather(gram_tile, "row", axis=0, tiled=True),
        preferred_element_type=jnp.float32,
    )
    poly_tile = (QUINTIC_B * gram_tile.astype(jnp.float32) + QUINTIC_C * square).astype(
        jnp.bfloat16
    )
    product = lax.dot_general(
        lax.all_gather(poly_tile, "row", axis=0, tiled=True),
        column_slab,
        COLS_BY_ROWS,
        preferred_element_type=jnp.float32,
    )
    return QUINTIC_A * iterate.astype(jnp.float32) + product


def polynomial_kernel(
    depth, inverse, x_ref, slab_out, poly_out,
    slab, part, paired, outgoing, incoming, turned, gram, panel, poly,
    x_send, x_recv, pair_send, pair_recv, sum_send, sum_recv,
    hop_send, hop_recv, side_send, side_recv, panel_send, panel_recv, turn_sem, out_sem,
):
    m = x_ref.shape[0]
    h, s = m // 2, m // (2 * depth)
    c, r = lax.axis_index("col"), lax.axis_index("row")
    z = r // 2
    core = r % 2
    side = r + 1 - 2 * core
    across = {1: c + 1 - 2 * (c % 2), 2: (c + 2) % 4, 3: 3 - c}
    lo, hi = pl.ds(0, h), pl.ds(h, h)

    def remote(source, target, send, recv, row=r, col=c):
        return pltpu.make_async_remote_copy(
            src_ref=source, dst_ref=target, send_sem=send, recv_sem=recv,
            device_id={"row": row, "col": col}, device_id_type=pl.DeviceIdType.MESH,
        )

    barrier = pltpu.get_barrier_semaphore()
    partners = [(r, across[l]) for l in (1, 2, 3)] + [(side, c)]
    partners += [(2 * ((z + d) % depth) + core, c) for d in range(1, depth)]
    for row, col in partners:
        pl.semaphore_signal(
            barrier, inc=1, device_id={"row": row, "col": col},
            device_id_type=pl.DeviceIdType.MESH,
        )
    pl.semaphore_wait(barrier, len(partners))

    def x_copy(i):
        source, block, half, bit = [
            (x_ref, 0, lo, 1),
            (x_ref, 1, hi, 2),
            (x_ref, 0, hi, 1),
            (x_ref, 1, lo, 2),
            (slab.at[0], 2, lo, 2),
            (slab.at[1], 2, hi, 1),
        ][i]
        return remote(
            source.at[half], slab.at[block, half], x_send.at[i], x_recv.at[i], col=across[bit]
        )

    def keep(k):
        source = x_ref if k == 0 else slab.at[k - 1]
        return pltpu.make_async_copy(source, slab_out.at[k], out_sem.at[k])

    def pair_copy(k):
        return remote(
            part.at[k % 2, 1 - core], paired.at[k], pair_send.at[k], pair_recv.at[k], row=side
        )

    def products(k):
        def step(i, carry):
            rows = pl.ds(pl.multiple_of(i * 2 * s, 2 * s), 2 * s)
            block = x_ref[rows] if k == 0 else slab[k - 1 if k < 3 else 0, rows]
            other = x_ref[...] if k < 3 else slab[1]
            total = inverse * lax.dot_general(
                block, other, ROWS_BY_ROWS, preferred_element_type=jnp.float32
            )
            part[k % 2, 0, i] = total[:s]
            part[k % 2, 1, i] = total[s:]
            return carry

        lax.fori_loop(0, depth, step, 0)
        pair_copy(k).start()

    def sum_copy(k, d):
        there = (z + d) % depth
        return remote(
            outgoing.at[k, there], incoming.at[k, d - 1],
            sum_send.at[k, d - 1], sum_recv.at[k, d - 1], row=2 * there + core,
        )

    def send_sums(k):
        pair_copy(k).wait_recv()

        def step(i, carry):
            total = part[k % 2, core, i] + paired[k, i]
            paired[k, i] = total
            outgoing[k, i] = total.astype(jnp.bfloat16)
            return carry

        lax.fori_loop(0, depth, step, 0)
        for d in range(1, depth):
            sum_copy(k, d).start()

    def panel_copy(k, l):
        return remote(
            gram.at[k, r], panel.at[l, k ^ l],
            panel_send.at[k, l - 1], panel_recv.at[k, l - 1], col=across[l],
        )

    def finish_sums(k):
        total = paired[k, z]
        for d in range(1, depth):
            sum_copy(k, d).wait_recv()
            total += incoming[k, d - 1].astype(jnp.float32)
        total = total.astype(jnp.bfloat16)
        if k < 3:
            gram[k, r] = total
            share(k)
        else:
            turned[...] = total
            turn_copy().start()

    def turn_copy():
        return remote(turned, gram.at[3, r], turn_sem.at[0], turn_sem.at[1], col=across[2])

    def share(k):
        panel[0, k] = gram[k, r]
        spread(0, gram, k)
        for l in (1, 2, 3):
            panel_copy(k, l).start()

    def hop(g, buffer, k, way, d):
        source = r - 2 * (d - 1) if way == 0 else r + 2 * (d - 1)
        target = r + 2 if way == 0 else r - 2
        return remote(
            buffer.at[k, source], buffer.at[k, source],
            hop_send.at[g, k, way, d - 1], hop_recv.at[g, k, way, d - 1], row=target,
        )

    def sends(way, d):
        if way == 0:
            return jnp.logical_and(z - (d - 1) >= 0, z <= depth - 2)
        return jnp.logical_and(z + (d - 1) <= depth - 1, z >= 1)

    def gets(way, d):
        return z - d >= 0 if way == 0 else z + d <= depth - 1

    def side_copy(g, buffer, k, way, d):
        source = r - 2 * d if way == 0 else r + 2 * d
        slot = d if way == 0 else depth - 1 + d
        return remote(
            buffer.at[k, source], buffer.at[k, source],
            side_send.at[g, k, slot], side_recv.at[g, k, slot], row=side,
        )

    def side_arrival(g, buffer, k, way, d):
        source = side - 2 * d if way == 0 else side + 2 * d
        slot = d if way == 0 else depth - 1 + d
        return remote(
            buffer.at[k, source], buffer.at[k, source],
            side_send.at[g, k, slot], side_recv.at[g, k, slot], row=side,
        )

    def arrival(g, buffer, k, way, d):
        source = r - 2 * d if way == 0 else r + 2 * d
        return remote(
            buffer.at[k, source], buffer.at[k, source],
            hop_send.at[g, k, way, d - 1], hop_recv.at[g, k, way, d - 1], row=side,
        )

    def spread(g, buffer, k):
        for way in (0, 1):
            pl.when(sends(way, 1))(lambda way=way: hop(g, buffer, k, way, 1).start())
        side_copy(g, buffer, k, 0, 0).start()

    def pass_on(g, buffer, k, d):
        for way in (0, 1):

            @pl.when(gets(way, d))
            def _(way=way):
                arrival(g, buffer, k, way, d).wait_recv()
                side_copy(g, buffer, k, way, d).start()

            if d < depth - 1:
                pl.when(sends(way, d + 1))(lambda way=way: hop(g, buffer, k, way, d + 1).start())

    def gathered(g, buffer, k):
        side_arrival(g, buffer, k, 0, 0).wait_recv()
        for way in (0, 1):
            for d in range(1, depth):
                pl.when(gets(way, d))(
                    lambda way=way, d=d: side_arrival(g, buffer, k, way, d).wait_recv()
                )

    def spread_sent(g, buffer, k):
        side_copy(g, buffer, k, 0, 0).wait_send()
        for way in (0, 1):
            for d in range(1, depth):
                pl.when(gets(way, d))(
                    lambda way=way, d=d: side_copy(g, buffer, k, way, d).wait_send()
                )
                pl.when(sends(way, d))(
                    lambda way=way, d=d: hop(g, buffer, k, way, d).wait_send()
                )

    x_copy(0).start()
    x_copy(1).start()
    keep(0).start()
    products(0)
    send_sums(0)
    for i in (0, 1):
        x_copy(i).wait()
    x_copy(2).start()
    x_copy(3).start()
    finish_sums(0)
    for d in range(1, depth):
        pass_on(0, gram, 0, d)
    for i in (2, 3):
        x_copy(i).wait()
    keep(1).start()
    keep(2).start()
    products(1)
    send_sums(1)
    pair_copy(0).wait_send()
    products(2)
    send_sums(2)
    pair_copy(1).wait_send()
    products(3)
    finish_sums(1)
    send_sums(3)
    pass_on(0, gram, 1, 1)
    finish_sums(2)
    for d in range(2, depth):
        pass_on(0, gram, 1, d)
    pass_on(0, gram, 2, 1)
    finish_sums(3)
    for d in range(2, depth):
        pass_on(0, gram, 2, d)
    turn_copy().wait()
    share(3)
    for d in range(1, depth):
        pass_on(0, gram, 3, d)
    for k in range(4):
        for l in (1, 2, 3):
            panel_copy(k, l).wait_recv()
    x_copy(4).start()
    x_copy(5).start()
    for k in range(4):
        gathered(0, gram, k)

    for first in (0, 2):
        square = jnp.zeros((2 * s, m), jnp.float32)
        for l in range(4):
            square += jnp.dot(
                panel[l, first : first + 2].reshape(2 * s, m),
                gram[l].reshape(m, m),
                preferred_element_type=jnp.float32,
            )
        for k in (first, first + 1):
            own = panel[0, k].astype(jnp.float32)
            rows = square[(k - first) * s : (k - first + 1) * s]
            poly[k, r] = (QUINTIC_B * own + QUINTIC_C * rows).astype(jnp.bfloat16)
            spread(1, poly, k)
    for d in range(1, depth):
        for k in range(4):
            pass_on(1, poly, k, d)
    for i in (4, 5):
        x_copy(i).wait()
    keep(3).start()
    for k in range(4):
        gathered(1, poly, k)
        pltpu.make_async_copy(poly.at[k], poly_out.at[k], out_sem.at[4 + k]).start()

    for k in range(4):
        if k > 1:
            pair_copy(k).wait_send()
        for d in range(1, depth):
            sum_copy(k, d).wait_send()
        for l in (1, 2, 3):
            panel_copy(k, l).wait_send()
        spread_sent(0, gram, k)
        spread_sent(1, poly, k)
        keep(k).wait()
        pltpu.make_async_copy(poly.at[k], poly_out.at[k], out_sem.at[4 + k]).wait()


def square_of_four(rows, iterate):
    m, n = iterate.shape
    depth, s = rows // 2, m // rows
    bf16, f32, dma = jnp.bfloat16, jnp.float32, pltpu.SemaphoreType.DMA
    slab, poly = pl.pallas_call(
        functools.partial(polynomial_kernel, depth, 1.0 / N),
        out_shape=(
            jax.ShapeDtypeStruct((4, m, n), bf16),
            jax.ShapeDtypeStruct((4, rows, s, m), bf16),
        ),
        in_specs=[pl.BlockSpec(memory_space=pltpu.VMEM)],
        out_specs=(pl.BlockSpec(memory_space=pl.ANY), pl.BlockSpec(memory_space=pl.ANY)),
        scratch_shapes=[
            pltpu.VMEM((3, m, n), bf16),
            pltpu.VMEM((2, 2, depth, s, m), f32),
            pltpu.VMEM((4, depth, s, m), f32),
            pltpu.VMEM((4, depth, s, m), bf16),
            pltpu.VMEM((4, depth - 1, s, m), bf16),
            pltpu.VMEM((s, m), bf16),
            pltpu.VMEM((4, rows, s, m), bf16),
            pltpu.VMEM((4, 4, s, m), bf16),
            pltpu.VMEM((4, rows, s, m), bf16),
            dma((6,)), dma((6,)),
            dma((4,)), dma((4,)),
            dma((4, depth - 1)), dma((4, depth - 1)),
            dma((2, 4, 2, depth - 1)), dma((2, 4, 2, depth - 1)),
            dma((2, 4, rows - 1)), dma((2, 4, rows - 1)),
            dma((4, 3)), dma((4, 3)),
            dma((2,)),
            dma((8,)),
        ],
        compiler_params=pltpu.CompilerParams(
            collective_id=0, has_side_effects=True, vmem_limit_bytes=VMEM_LIMIT
        ),
    )(iterate)
    product = lax.dot_general(
        poly.reshape(4 * m, m), slab.reshape(4 * m, n), COLS_BY_ROWS, preferred_element_type=f32
    )
    return QUINTIC_A * iterate.astype(f32) + product


def solution(mesh):
    rows, cols = mesh.shape["row"], mesh.shape["col"]
    placed = (P("col", "row"),)

    def local(iterate):
        m, n = iterate.shape
        if cols == 4 and rows % 2 == 0 and m % (16 * rows) == 0 and 30 * m * m + 10 * m * n < VMEM_LIMIT:
            return square_of_four(rows, iterate)
        return general(iterate)

    return jax.shard_map(
        local, mesh=mesh, in_specs=placed, out_specs=P("col", "row"), check_vma=False
    )
```

```python
import functools

import jax
import jax.numpy as jnp
from jax import lax
from jax.experimental import pallas as pl
from jax.experimental.pallas import tpu as pltpu
from jax.sharding import PartitionSpec as P

N = 18432


QUINTIC_A = 3.4445
QUINTIC_B = -4.775
QUINTIC_C = 2.0315

VMEM_LIMIT = 63 * 2**20
ROWS_BY_ROWS = (((1,), (1,)), ((), ()))
COLS_BY_ROWS = (((0,), (0,)), ((), ()))


def general(iterate):
    inverse = 1.0 / N
    column_slab = lax.all_gather(iterate, "col", axis=0, tiled=True)
    gram_total = lax.psum_scatter(
        lax.dot_general(column_slab, iterate, ROWS_BY_ROWS, preferred_element_type=jnp.float32),
        "row",
        scatter_dimension=0,
        tiled=True,
    )
    gram_tile = (gram_total * inverse).astype(jnp.bfloat16)
    row_panel = lax.all_gather(gram_tile, "col", axis=1, tiled=True)
    square = jnp.dot(
        row_panel,
        lax.all_gather(gram_tile, "row", axis=0, tiled=True),
        preferred_element_type=jnp.float32,
    )
    poly_tile = (QUINTIC_B * gram_tile.astype(jnp.float32) + QUINTIC_C * square).astype(
        jnp.bfloat16
    )
    product = lax.dot_general(
        lax.all_gather(poly_tile, "row", axis=0, tiled=True),
        column_slab,
        COLS_BY_ROWS,
        preferred_element_type=jnp.float32,
    )
    return QUINTIC_A * iterate.astype(jnp.float32) + product


def polynomial_kernel(
    depth, inverse, x_ref, slab_out, poly_out, total_out,
    slab, total, part, paired, outgoing, incoming, turned, gram, panel, poly,
    x_send, x_recv, pair_send, pair_recv, sum_send, sum_recv,
    hop_send, hop_recv, side_send, side_recv, panel_send, panel_recv, turn_sem, out_sem,
):
    m = x_ref.shape[0]
    h, s = m // 2, m // (2 * depth)
    c, r = lax.axis_index("col"), lax.axis_index("row")
    z = r // 2
    core = r % 2
    side = r + 1 - 2 * core
    across = {1: c + 1 - 2 * (c % 2), 2: (c + 2) % 4, 3: 3 - c}
    lo, hi = pl.ds(0, h), pl.ds(h, h)

    def remote(source, target, send, recv, row=r, col=c):
        return pltpu.make_async_remote_copy(
            src_ref=source, dst_ref=target, send_sem=send, recv_sem=recv,
            device_id={"row": row, "col": col}, device_id_type=pl.DeviceIdType.MESH,
        )

    barrier = pltpu.get_barrier_semaphore()
    partners = [(r, across[l]) for l in (1, 2, 3)] + [(side, c)]
    partners += [(2 * ((z + d) % depth) + core, c) for d in range(1, depth)]
    for row, col in partners:
        pl.semaphore_signal(
            barrier, inc=1, device_id={"row": row, "col": col},
            device_id_type=pl.DeviceIdType.MESH,
        )
    pl.semaphore_wait(barrier, len(partners))

    def x_copy(i):
        source, block, half, bit = [
            (x_ref, 0, lo, 1),
            (x_ref, 1, hi, 2),
            (x_ref, 0, hi, 1),
            (x_ref, 1, lo, 2),
            (slab.at[0], 2, lo, 2),
            (slab.at[1], 2, hi, 1),
        ][i]
        return remote(
            source.at[half], slab.at[block, half], x_send.at[i], x_recv.at[i], col=across[bit]
        )

    def keep(i):
        source = (slab.at[2], poly.at[3], total)[i]
        return pltpu.make_async_copy(source, (slab_out, poly_out, total_out)[i], out_sem.at[i])

    def product(k):
        source = x_ref if k == 0 else slab.at[k - 1]
        width = 256 if source.shape[1] % 256 == 0 else source.shape[1]
        outgoing[0:2] = poly[k].reshape(m, m).T.reshape(2, depth, s, m)

        def step(i, carry):
            columns = pl.ds(pl.multiple_of(i * width, width), width)
            term = jnp.dot(
                outgoing[0:2].reshape(m, m), source[:, columns], preferred_element_type=jnp.float32
            )
            if k == 0:
                total[:, columns] = QUINTIC_A * x_ref[:, columns].astype(jnp.float32) + term
            else:
                total[:, columns] += term
            return carry

        lax.fori_loop(0, source.shape[1] // width, step, 0)

    def pair_copy(k):
        return remote(
            part.at[k % 2, 1 - core], paired.at[k], pair_send.at[k], pair_recv.at[k], row=side
        )

    def products(k):
        def step(i, carry):
            rows = pl.ds(pl.multiple_of(i * 2 * s, 2 * s), 2 * s)
            block = x_ref[rows] if k == 0 else slab[k - 1 if k < 3 else 0, rows]
            other = x_ref[...] if k < 3 else slab[1]
            block_sum = inverse * lax.dot_general(
                block, other, ROWS_BY_ROWS, preferred_element_type=jnp.float32
            )
            part[k % 2, 0, i] = block_sum[:s]
            part[k % 2, 1, i] = block_sum[s:]
            return carry

        lax.fori_loop(0, depth, step, 0)
        pair_copy(k).start()

    def sum_copy(k, d):
        there = (z + d) % depth
        return remote(
            outgoing.at[k, there], incoming.at[k, d - 1],
            sum_send.at[k, d - 1], sum_recv.at[k, d - 1], row=2 * there + core,
        )

    def send_sums(k):
        pair_copy(k).wait_recv()

        def step(i, carry):
            block_sum = part[k % 2, core, i] + paired[k, i]
            paired[k, i] = block_sum
            outgoing[k, i] = block_sum.astype(jnp.bfloat16)
            return carry

        lax.fori_loop(0, depth, step, 0)
        for d in range(1, depth):
            sum_copy(k, d).start()

    def panel_copy(k, l):
        return remote(
            gram.at[k, r], panel.at[l, k ^ l],
            panel_send.at[k, l - 1], panel_recv.at[k, l - 1], col=across[l],
        )

    def finish_sums(k):
        tile = paired[k, z]
        for d in range(1, depth):
            sum_copy(k, d).wait_recv()
            tile += incoming[k, d - 1].astype(jnp.float32)
        tile = tile.astype(jnp.bfloat16)
        if k < 3:
            gram[k, r] = tile
            share(k)
        else:
            turned[...] = tile
            turn_copy().start()

    def turn_copy():
        return remote(turned, gram.at[3, r], turn_sem.at[0], turn_sem.at[1], col=across[2])

    def share(k):
        panel[0, k] = gram[k, r]
        spread(0, gram, k)
        for l in (1, 2, 3):
            panel_copy(k, l).start()

    def hop(g, buffer, k, way, d):
        source = r - 2 * (d - 1) if way == 0 else r + 2 * (d - 1)
        target = r + 2 if way == 0 else r - 2
        return remote(
            buffer.at[k, source], buffer.at[k, source],
            hop_send.at[g, k, way, d - 1], hop_recv.at[g, k, way, d - 1], row=target,
        )

    def sends(way, d):
        if way == 0:
            return jnp.logical_and(z - (d - 1) >= 0, z <= depth - 2)
        return jnp.logical_and(z + (d - 1) <= depth - 1, z >= 1)

    def gets(way, d):
        return z - d >= 0 if way == 0 else z + d <= depth - 1

    def side_copy(g, buffer, k, way, d):
        source = r - 2 * d if way == 0 else r + 2 * d
        slot = d if way == 0 else depth - 1 + d
        return remote(
            buffer.at[k, source], buffer.at[k, source],
            side_send.at[g, k, slot], side_recv.at[g, k, slot], row=side,
        )

    def side_arrival(g, buffer, k, way, d):
        source = side - 2 * d if way == 0 else side + 2 * d
        slot = d if way == 0 else depth - 1 + d
        return remote(
            buffer.at[k, source], buffer.at[k, source],
            side_send.at[g, k, slot], side_recv.at[g, k, slot], row=side,
        )

    def arrival(g, buffer, k, way, d):
        source = r - 2 * d if way == 0 else r + 2 * d
        return remote(
            buffer.at[k, source], buffer.at[k, source],
            hop_send.at[g, k, way, d - 1], hop_recv.at[g, k, way, d - 1], row=side,
        )

    def spread(g, buffer, k):
        for way in (0, 1):
            pl.when(sends(way, 1))(lambda way=way: hop(g, buffer, k, way, 1).start())
        side_copy(g, buffer, k, 0, 0).start()

    def pass_on(g, buffer, k, d):
        for way in (0, 1):

            @pl.when(gets(way, d))
            def _(way=way):
                arrival(g, buffer, k, way, d).wait_recv()
                side_copy(g, buffer, k, way, d).start()

            if d < depth - 1:
                pl.when(sends(way, d + 1))(lambda way=way: hop(g, buffer, k, way, d + 1).start())

    def gathered(g, buffer, k):
        side_arrival(g, buffer, k, 0, 0).wait_recv()
        for way in (0, 1):
            for d in range(1, depth):
                pl.when(gets(way, d))(
                    lambda way=way, d=d: side_arrival(g, buffer, k, way, d).wait_recv()
                )

    def spread_sent(g, buffer, k):
        side_copy(g, buffer, k, 0, 0).wait_send()
        for way in (0, 1):
            for d in range(1, depth):
                pl.when(gets(way, d))(
                    lambda way=way, d=d: side_copy(g, buffer, k, way, d).wait_send()
                )
                pl.when(sends(way, d))(
                    lambda way=way, d=d: hop(g, buffer, k, way, d).wait_send()
                )

    x_copy(0).start()
    x_copy(1).start()
    products(0)
    send_sums(0)
    for i in (0, 1):
        x_copy(i).wait()
    x_copy(2).start()
    x_copy(3).start()
    finish_sums(0)
    for d in range(1, depth):
        pass_on(0, gram, 0, d)
    for i in (2, 3):
        x_copy(i).wait()
    products(1)
    send_sums(1)
    pair_copy(0).wait_send()
    products(2)
    send_sums(2)
    pair_copy(1).wait_send()
    products(3)
    finish_sums(1)
    send_sums(3)
    pass_on(0, gram, 1, 1)
    finish_sums(2)
    for d in range(2, depth):
        pass_on(0, gram, 1, d)
    pass_on(0, gram, 2, 1)
    finish_sums(3)
    for d in range(2, depth):
        pass_on(0, gram, 2, d)
    turn_copy().wait()
    share(3)
    for d in range(1, depth):
        pass_on(0, gram, 3, d)
    for k in range(4):
        for l in (1, 2, 3):
            panel_copy(k, l).wait_recv()
    x_copy(4).start()
    x_copy(5).start()
    for k in range(4):
        gathered(0, gram, k)

    for first in (0, 2):
        square = jnp.zeros((2 * s, m), jnp.float32)
        for l in range(4):
            square += jnp.dot(
                panel[l, first : first + 2].reshape(2 * s, m),
                gram[l].reshape(m, m),
                preferred_element_type=jnp.float32,
            )
        for k in (first, first + 1):
            own = panel[0, k].astype(jnp.float32)
            rows = square[(k - first) * s : (k - first + 1) * s]
            poly[k, r] = (QUINTIC_B * own + QUINTIC_C * rows).astype(jnp.bfloat16)
            spread(1, poly, k)
    for k in range(4):
        for d in range(1, depth):
            sum_copy(k, d).wait_send()
    last = depth - 1
    for wave in range(1, 4 + last):
        for d in range(last, 0, -1):
            if 0 <= wave - d < 4:
                pass_on(1, poly, wave - d, d)
        k = wave - last - 1
        if 0 <= k < 3:
            gathered(1, poly, k)
            product(k)
    keep(2).start()
    for i in (4, 5):
        x_copy(i).wait()
    keep(0).start()
    gathered(1, poly, 3)
    keep(1).start()

    for k in range(4):
        if k > 1:
            pair_copy(k).wait_send()
        for l in (1, 2, 3):
            panel_copy(k, l).wait_send()
        spread_sent(0, gram, k)
        spread_sent(1, poly, k)
    for i in range(3):
        keep(i).wait()


def square_of_four(rows, iterate):
    m, n = iterate.shape
    depth, s = rows // 2, m // rows
    bf16, f32, dma = jnp.bfloat16, jnp.float32, pltpu.SemaphoreType.DMA
    slab, poly, total = pl.pallas_call(
        functools.partial(polynomial_kernel, depth, 1.0 / N),
        out_shape=(
            jax.ShapeDtypeStruct((m, n), bf16),
            jax.ShapeDtypeStruct((rows, s, m), bf16),
            jax.ShapeDtypeStruct((m, n), f32),
        ),
        in_specs=[pl.BlockSpec(memory_space=pltpu.VMEM)],
        out_specs=(pl.BlockSpec(memory_space=pl.ANY),) * 3,
        scratch_shapes=[
            pltpu.VMEM((3, m, n), bf16),
            pltpu.VMEM((m, n), f32),
            pltpu.VMEM((2, 2, depth, s, m), f32),
            pltpu.VMEM((4, depth, s, m), f32),
            pltpu.VMEM((4, depth, s, m), bf16),
            pltpu.VMEM((4, depth - 1, s, m), bf16),
            pltpu.VMEM((s, m), bf16),
            pltpu.VMEM((4, rows, s, m), bf16),
            pltpu.VMEM((4, 4, s, m), bf16),
            pltpu.VMEM((4, rows, s, m), bf16),
            dma((6,)), dma((6,)),
            dma((4,)), dma((4,)),
            dma((4, depth - 1)), dma((4, depth - 1)),
            dma((2, 4, 2, depth - 1)), dma((2, 4, 2, depth - 1)),
            dma((2, 4, rows - 1)), dma((2, 4, rows - 1)),
            dma((4, 3)), dma((4, 3)),
            dma((2,)),
            dma((3,)),
        ],
        compiler_params=pltpu.CompilerParams(
            collective_id=0, has_side_effects=True, vmem_limit_bytes=VMEM_LIMIT
        ),
    )(iterate)
    product = lax.dot_general(poly.reshape(m, m), slab, COLS_BY_ROWS, preferred_element_type=f32)
    return total + product


def solution(mesh):
    rows, cols = mesh.shape["row"], mesh.shape["col"]
    placed = (P("col", "row"),)

    def local(iterate):
        m, n = iterate.shape
        if cols == 4 and rows % 2 == 0 and m % (16 * rows) == 0 and 43 * m * m + 12 * m * n < VMEM_LIMIT:
            return square_of_four(rows, iterate)
        return general(iterate)

    return jax.shard_map(
        local, mesh=mesh, in_specs=placed, out_specs=P("col", "row"), check_vma=False
    )
```
